512 devices in a mesh: ctx: 64 (over x, y, core), tp: 8 (over z).
Axes of the slice: x: 4, y: 8, z: 8, core: 2. Of those that a mesh axis runs over, the one named last changes fastest.
Arguments:
- queries: bfloat16 [32768, 2048], P('ctx', 'tp'), may hold values from -1.75 to 1.75
- keys: bfloat16 [32768, 2048], P('ctx', 'tp'), may hold values from -1.75 to 1.75
- values: bfloat16 [32768, 2048], P('ctx', 'tp'), may hold values from -18 to 18
- gain: bfloat16 [2048], P('tp'), may hold values from 0.099609375 to 1.8984375
- cotangent: bfloat16 [32768, 2048], P('ctx', 'tp'), may hold values from -6 to 6
Outputs:
- normed: bfloat16 [32768, 2048], P('ctx', 'tp')
- grad_queries: bfloat16 [32768, 2048], P('ctx', 'tp')
- grad_keys: bfloat16 [32768, 2048], P('ctx', 'tp')
- grad_values: bfloat16 [32768, 2048], P('ctx', 'tp')
The draws below stay inside these ranges and needn't reach their ends.
All inputs are finite; a program needn't handle non-finite values.
Results may differ from the reference program's by a relative error of at most 0.0058.
Values sent between devices are 32-bit elements; how exact they have to be, the bound alone decides.
A program may use at most 64 MiB of HBM per device.

```python
import jax
import jax.numpy as jnp
from jax import lax

HEAD = 128
HEADS = 16
TOK_DEV = 512
D = 2048
TOKENS = 32768
N_CTX = 64


def draw_values(key, part):
    head_place = jnp.arange(HEADS, dtype=jnp.float32) / max(HEADS - 1, 1)
    head_scale = 3.0 ** head_place
    noise = jnp.clip(jax.random.normal(key, (TOKENS, HEADS, HEAD), jnp.float32), -6.0, 6.0)
    return (noise * head_scale[None, :, None]).reshape(TOKENS, HEADS * HEAD).astype(jnp.bfloat16)


def level_of(key, extent, shards, smallest, top_value):
    factor_of = 1.0
    for dim, blocks in shards:
        steps = jax.random.uniform(jax.random.fold_in(jax.random.fold_in(key, 6), dim), (blocks,), jnp.float32, smallest / len(shards), top_value / len(shards))
        factor_of = factor_of * jnp.repeat(jnp.exp(steps), extent[dim] // blocks).reshape((-1,) + (1,) * (len(extent) - 1 - dim))
    return factor_of


def scatter_about(rng, shape, deviation, most, split=(), kind=jnp.bfloat16):
    values = deviation * jax.random.normal(rng, shape, jnp.float32)
    if split:
        values = values * level_of(rng, shape, split, -0.22, 0.18)
    return jnp.clip(values, -most, most).astype(kind)


def setup_inputs(seed: int = 0) -> dict:
    key_of = jax.random.split(jax.random.key(seed), 6)
    queries = scatter_about(key_of[0], (TOKENS, D), 0.3, 1.75, ((0, 64), (1, 8)))
    keys = scatter_about(key_of[1], (TOKENS, D), 0.3, 1.75, ((0, 64), (1, 8)))
    values = draw_values(jax.random.fold_in(key_of[5], 71), 0)
    gain = jnp.clip(1.0 + 0.18 * jax.random.normal(key_of[3], (D,), jnp.float32), 0.099609375, 1.8984375).astype(jnp.bfloat16)
    cotangent = scatter_about(key_of[4], (TOKENS, D), 1.0, 6.0, ((0, 64), (1, 8)))
    return dict(queries=queries, keys=keys, values=values, gain=gain, cotangent=cotangent)


epsilon = 1e-06

def split_heads(matrix):
    return matrix.reshape(matrix.shape[0], HEADS, HEAD).transpose(1, 0, 2).astype(jnp.float32)

def join_heads(tensor):
    return tensor.transpose(1, 0, 2).reshape(tensor.shape[1], HEADS * HEAD)

def reference(queries, keys, values, gain, cotangent):

    def to_blocks(matrix):
        return matrix.reshape(N_CTX, TOK_DEV, HEADS * HEAD)
    query_blocks = to_blocks(queries)
    key_blocks = to_blocks(keys)
    value_blocks = to_blocks(values)
    grad_blocks = to_blocks(cotangent)
    causal = jnp.tril(jnp.ones((TOK_DEV, TOK_DEV), jnp.bool_))
    gain_wide = gain.astype(jnp.float32)
    highest = lax.Precision.HIGHEST

    def state_of(members):
        key_now, value_now = members
        return jnp.einsum('hte,htf->hef', split_heads(key_now), split_heads(value_now), precision=highest)
    own_state = lax.map(state_of, (key_blocks, value_blocks))
    zero_state = jnp.zeros_like(own_state[:1])
    prior_state = jnp.concatenate([zero_state, jnp.cumsum(own_state, axis=0)[:-1]], axis=0)
    prior_low = prior_state.astype(jnp.bfloat16)

    def forward(members):
        query_now, key_now, value_now, grad_now, prior_now = members
        query_heads = split_heads(query_now)
        key_heads = split_heads(key_now)
        value_heads = split_heads(value_now)
        prior_wide = prior_now.astype(jnp.float32)
        masked = jnp.where(causal, jnp.einsum('hte,hse->hts', query_heads, key_heads, precision=highest), 0.0).astype(jnp.bfloat16)
        combined = jnp.einsum('hts,hse->hte', masked.astype(jnp.float32), value_heads, precision=highest)
        combined = combined + jnp.einsum('hte,hef->htf', query_heads, prior_wide, precision=highest)
        attended = join_heads(combined)
        inverse = lax.rsqrt(lax.optimization_barrier(jnp.mean(attended * attended, axis=-1)) + epsilon)
        normed = (attended * inverse[:, None] * gain_wide).astype(jnp.bfloat16)
        scaled = grad_now.astype(jnp.float32) * gain_wide
        mean_product = lax.optimization_barrier(jnp.mean(scaled * attended, axis=-1))
        grad_att = (inverse[:, None] * scaled - (inverse ** 3 * mean_product)[:, None] * attended).astype(jnp.bfloat16)
        grad_heads = split_heads(grad_att)
        cross_low = jnp.where(causal, jnp.einsum('hte,hse->hts', grad_heads, value_heads, precision=highest), 0.0).astype(jnp.bfloat16)
        grad_query = jnp.einsum('hts,hse->hte', cross_low.astype(jnp.float32), key_heads, precision=highest)
        grad_query = grad_query + jnp.einsum('htf,hef->hte', grad_heads, prior_wide, precision=highest)
        later_own = jnp.einsum('hte,htf->hef', query_heads, grad_heads, precision=highest)
        return (normed, grad_att, join_heads(grad_query).astype(jnp.bfloat16), later_own)
    normed, grad_att, grad_queries, later_own = lax.map(forward, (query_blocks, key_blocks, value_blocks, grad_blocks, prior_low))
    reversed_sums = jnp.cumsum(later_own[::-1], axis=0)[::-1]
    after_state = jnp.concatenate([reversed_sums[1:], jnp.zeros_like(reversed_sums[:1])], axis=0)
    after_low = after_state.astype(jnp.bfloat16)

    def backward(members):
        query_now, key_now, value_now, grad_now, after_now = members
        query_heads = split_heads(query_now)
        key_heads = split_heads(key_now)
        value_heads = split_heads(value_now)
        grad_heads = split_heads(grad_now)
        after_wide = after_now.astype(jnp.float32)
        masked = jnp.where(causal, jnp.einsum('hte,hse->hts', query_heads, key_heads, precision=highest), 0.0).astype(jnp.bfloat16)
        cross_low = jnp.where(causal, jnp.einsum('hte,hse->hts', grad_heads, value_heads, precision=highest), 0.0).astype(jnp.bfloat16)
        grad_key = jnp.einsum('hst,hse->hte', cross_low.astype(jnp.float32), query_heads, precision=highest)
        grad_key = grad_key + jnp.einsum('htf,hef->hte', value_heads, after_wide, precision=highest)
        grad_value = jnp.einsum('hst,hsf->htf', masked.astype(jnp.float32), grad_heads, precision=highest)
        grad_value = grad_value + jnp.einsum('hte,hef->htf', key_heads, after_wide, precision=highest)
        return (join_heads(grad_key).astype(jnp.bfloat16), join_heads(grad_value).astype(jnp.bfloat16))
    grad_keys, grad_values = lax.map(backward, (query_blocks, key_blocks, value_blocks, grad_att, after_low))

    def to_rows(tensor):
        return tensor.reshape(TOKENS, HEADS * HEAD)
    return (to_rows(normed), to_rows(grad_queries), to_rows(grad_keys), to_rows(grad_values))
```

```python
import jax
import jax.numpy as jnp
from jax import lax
from jax.experimental import pallas as pl
from jax.experimental.pallas import tpu as pltpu
from jax.sharding import PartitionSpec as P

HEAD = 128
HEADS = 16
D = HEAD * HEADS
ROW = 16
COLS = 4
TP = 8
T = 512
H = T // 2
W = 256
PIECE = 16
epsilon = 1e-06
F32 = jnp.float32
BF16 = jnp.bfloat16
MESH = pl.DeviceIdType.MESH

ROW_ORDER = (8, 7, 9, 6, 10, 5, 11, 4, 12, 3, 13, 2, 14, 1, 15)
COL_ORDER = (2, 1, 3)
TP_ORDER = (4, 3, 5, 2, 6, 1, 7)


def dot(a, b, ca, cb):
    return lax.dot_general(a, b, (((ca,), (cb,)), ((), ())), preferred_element_type=F32)


def kernel(
    q_in, k_in, v_in, gain_ref, c_in, n_out, dq_out, dk_out, dv_out,
    q, k, v, c, scaled, att, grad, m_top, m_low, x_top, x_low, dk_acc, dv_acc,
    n_buf, dq_buf, dk_buf, dv_buf, prior_bd, after_bd, stats,
    own_a, gath_a, tot_a, back_a, full_a, own_b, gath_b, tot_b, back_b, full_b,
    in_sem, out_sem, row_send_a, row_recv_a, col_send_a, col_recv_a, ret_send_a, ret_recv_a,
    row_send_b, row_recv_b, col_send_b, col_recv_b, ret_send_b, ret_recv_b, tp_send, tp_recv,
):
    me = lax.axis_index("ctx")
    z = lax.axis_index("tp")
    x = me // ROW
    r = me % ROW

    loads = [
        pltpu.make_async_copy(src, dst, in_sem.at[i])
        for i, (src, dst) in enumerate(((k_in, k), (v_in, v), (q_in, q), (c_in, c)))
    ]
    for load in loads:
        load.start()

    def row_peer(off):
        j = (r + off) % ROW
        return j, (x * ROW + j, z)

    def col_peer(off):
        return (((x + off) % COLS) * ROW + r, z)

    def tp_peer(off):
        return (me, (z + off) % TP)

    barrier = pltpu.get_barrier_semaphore()
    for off in ROW_ORDER:
        pl.semaphore_signal(barrier, inc=1, device_id=row_peer(off)[1], device_id_type=MESH)
    for off in COL_ORDER:
        pl.semaphore_signal(barrier, inc=1, device_id=col_peer(off), device_id_type=MESH)
    for off in TP_ORDER:
        pl.semaphore_signal(barrier, inc=1, device_id=tp_peer(off), device_id_type=MESH)

    prior_bd[...] = jnp.zeros_like(prior_bd)
    after_bd[...] = jnp.zeros_like(after_bd)

    def put_own(own, left, right):
        state = dot(left, right, 0, 0)
        own[0:HEAD, :] = state[0:HEAD, 0:HEAD]
        own[HEAD:W, :] = state[HEAD:W, HEAD:W]

    def row_copies(own, gath, send, recv):
        copies = []
        for off in ROW_ORDER:
            j, peer = row_peer(off)
            copies.append(
                pltpu.make_async_remote_copy(
                    src_ref=own.at[pl.ds(pl.multiple_of(j * PIECE, PIECE), PIECE)],
                    dst_ref=gath.at[r],
                    send_sem=send.at[off],
                    recv_sem=recv.at[off],
                    device_id=peer,
                    device_id_type=MESH,
                )
            )
        return copies

    def col_copies(tot, send, recv):
        return [
            pltpu.make_async_remote_copy(
                src_ref=tot.at[x],
                dst_ref=tot.at[x],
                send_sem=send.at[off],
                recv_sem=recv.at[off],
                device_id=col_peer(off),
                device_id_type=MESH,
            )
            for off in COL_ORDER
        ]

    def ret_copies(back, full, send, recv):
        copies = []
        for off in ROW_ORDER:
            j, peer = row_peer(off)
            copies.append(
                pltpu.make_async_remote_copy(
                    src_ref=back.at[j],
                    dst_ref=full.at[r],
                    send_sem=send.at[off],
                    recv_sem=recv.at[off],
                    device_id=peer,
                    device_id_type=MESH,
                )
            )
        return copies

    def start(copies):
        for copy in copies:
            copy.start()

    def received(copies):
        for copy in copies:
            copy.wait_recv()

    def sent(copies):
        for copy in copies:
            copy.wait_send()

    def scan_row(own, gath, tot, reverse):
        gath[r] = own[pl.ds(pl.multiple_of(r * PIECE, PIECE), PIECE), :]
        run = jnp.zeros((PIECE, HEAD), F32)
        before = [None] * ROW
        for j in reversed(range(ROW)) if reverse else range(ROW):
            before[j] = run
            run = run + gath[j]
        tot[x] = run
        return before

    def scan_back(before, tot, back, full, reverse):
        base = jnp.zeros((PIECE, HEAD), F32)
        for other in range(COLS):
            counts = (other > x) if reverse else (other < x)
            base = base + jnp.where(counts, tot[other], 0.0)
        for j in range(ROW):
            back[j] = before[j] + base

    loads[0].wait()
    loads[1].wait()
    put_own(own_a, k[...], v[...])
    pl.semaphore_wait(barrier, len(ROW_ORDER) + len(COL_ORDER) + len(TP_ORDER))
    row_a = row_copies(own_a, gath_a, row_send_a, row_recv_a)
    start(row_a)

    loads[2].wait()
    loads[3].wait()
    lower = lax.broadcasted_iota(jnp.int32, (H, H), 0) >= lax.broadcasted_iota(jnp.int32, (H, H), 1)

    def masked_products(left, right, top, low):
        for h in range(2):
            cols = slice(h * HEAD, (h + 1) * HEAD)
            top[h] = jnp.where(lower, dot(left[0:H, cols], right[0:H, cols], 1, 1), 0.0).astype(BF16)
            low[h, :, 0:H] = dot(left[H:T, cols], right[0:H, cols], 1, 1).astype(BF16)
            low[h, :, H:T] = jnp.where(
                lower, dot(left[H:T, cols], right[H:T, cols], 1, 1), 0.0
            ).astype(BF16)

    masked_products(q, k, m_top, m_low)
    for h in range(2):
        cols = slice(h * HEAD, (h + 1) * HEAD)
        att[0:H, cols] = dot(m_top[h], v[0:H, cols], 1, 0)
        att[H:T, cols] = dot(m_low[h], v[:, cols], 1, 0)
    gain = gain_ref[...].astype(F32)
    scaled[...] = c[...].astype(F32) * gain

    received(row_a)
    before = scan_row(own_a, gath_a, tot_a, False)
    col_a = col_copies(tot_a, col_send_a, col_recv_a)
    start(col_a)
    received(col_a)
    scan_back(before, tot_a, back_a, full_a, False)
    ret_a = ret_copies(back_a, full_a, ret_send_a, ret_recv_a)
    start(ret_a)
    full_a[r] = back_a[r]
    received(ret_a)

    def put_bd(bd, full):
        low_state = full[...].reshape(W, HEAD).astype(BF16)
        bd[0:HEAD, 0:HEAD] = low_state[0:HEAD]
        bd[HEAD:W, HEAD:W] = low_state[HEAD:W]

    put_bd(prior_bd, full_a)
    att[...] += dot(q[...], prior_bd[...], 1, 0)

    eye = lax.broadcasted_iota(jnp.int32, (HEAD, HEAD), 0) == lax.broadcasted_iota(
        jnp.int32, (HEAD, HEAD), 1
    )
    rows = []
    for kind in range(2):
        for a in range(T // HEAD):
            part = att[a * HEAD:(a + 1) * HEAD, :]
            other = part if kind == 0 else scaled[a * HEAD:(a + 1) * HEAD, :]
            product = part * other
            sums = jnp.sum(product[:, 0:HEAD] + product[:, HEAD:W], axis=1, keepdims=True)
            rows.append(jnp.sum(jnp.where(eye, sums, 0.0), axis=0, keepdims=True))
    stats[z] = jnp.concatenate(rows, axis=0)
    tp_copies = [
        pltpu.make_async_remote_copy(
            src_ref=stats.at[z],
            dst_ref=stats.at[z],
            send_sem=tp_send.at[off],
            recv_sem=tp_recv.at[off],
            device_id=tp_peer(off),
            device_id_type=MESH,
        )
        for off in TP_ORDER
    ]
    start(tp_copies)
    received(tp_copies)
    totals = jnp.sum(stats[...], axis=0)
    inverse_row = lax.rsqrt(totals[0:4] / D + epsilon)
    coef_row = inverse_row * inverse_row * inverse_row * (totals[4:8] / D)

    def column(row):
        return jnp.sum(jnp.where(eye, row, 0.0), axis=1, keepdims=True)

    inverse = []
    for a in range(T // HEAD):
        span = slice(a * HEAD, (a + 1) * HEAD)
        inverse.append(column(inverse_row[a:a + 1]))
        coef = column(coef_row[a:a + 1])
        grad[span, :] = (inverse[a] * scaled[span, :] - coef * att[span, :]).astype(BF16)

    put_own(own_b, q[...], grad[...])
    row_b = row_copies(own_b, gath_b, row_send_b, row_recv_b)
    start(row_b)

    for a in range(T // HEAD):
        span = slice(a * HEAD, (a + 1) * HEAD)
        n_buf[span, :] = (att[span, :] * inverse[a] * gain).astype(BF16)
    stores = [pltpu.make_async_copy(n_buf, n_out, out_sem.at[0])]
    stores[0].start()
    masked_products(grad, v, x_top, x_low)

    received(row_b)
    before = scan_row(own_b, gath_b, tot_b, True)
    col_b = col_copies(tot_b, col_send_b, col_recv_b)
    start(col_b)
    for h in range(2):
        cols = slice(h * HEAD, (h + 1) * HEAD)
        dk_acc[0:H, cols] = dot(x_top[h], q[0:H, cols], 0, 0) + dot(x_low[h, :, 0:H], q[H:T, cols], 0, 0)
        dk_acc[H:T, cols] = dot(x_low[h, :, H:T], q[H:T, cols], 0, 0)
    received(col_b)
    scan_back(before, tot_b, back_b, full_b, True)
    ret_b = ret_copies(back_b, full_b, ret_send_b, ret_recv_b)
    start(ret_b)
    full_b[r] = back_b[r]

    for h in range(2):
        cols = slice(h * HEAD, (h + 1) * HEAD)
        dv_acc[0:H, cols] = dot(m_top[h], grad[0:H, cols], 0, 0) + dot(
            m_low[h, :, 0:H], grad[H:T, cols], 0, 0
        )
        dv_acc[H:T, cols] = dot(m_low[h, :, H:T], grad[H:T, cols], 0, 0)
    for h in range(2):
        cols = slice(h * HEAD, (h + 1) * HEAD)
        from_prior = dot(grad[:, cols], prior_bd[cols, cols], 1, 1)
        dq_buf[0:H, cols] = (dot(x_top[h], k[0:H, cols], 1, 0) + from_prior[0:H]).astype(BF16)
        dq_buf[H:T, cols] = (dot(x_low[h], k[:, cols], 1, 0) + from_prior[H:T]).astype(BF16)
    stores.append(pltpu.make_async_copy(dq_buf, dq_out, out_sem.at[1]))
    stores[1].start()
    for copies in (row_a, col_a, ret_a, tp_copies, row_b, col_b):
        sent(copies)

    received(ret_b)
    put_bd(after_bd, full_b)
    dk_buf[...] = (dk_acc[...] + dot(v[...], after_bd[...], 1, 1)).astype(BF16)
    stores.append(pltpu.make_async_copy(dk_buf, dk_out, out_sem.at[2]))
    stores[2].start()
    dv_buf[...] = (dv_acc[...] + dot(k[...], after_bd[...], 1, 0)).astype(BF16)
    stores.append(pltpu.make_async_copy(dv_buf, dv_out, out_sem.at[3]))
    stores[3].start()
    sent(ret_b)
    for store in stores:
        store.wait()


def shards(queries, keys, values, gain, cotangent):
    block = jax.ShapeDtypeStruct((T, W), BF16)
    anywhere = pl.BlockSpec(memory_space=pl.ANY)
    low = pltpu.VMEM((T, W), BF16)
    wide = pltpu.VMEM((T, W), F32)
    dma = pltpu.SemaphoreType.DMA
    scan_buffers = [
        pltpu.VMEM((W, HEAD), F32),
        pltpu.VMEM((ROW, PIECE, HEAD), F32),
        pltpu.VMEM((COLS, PIECE, HEAD), F32),
        pltpu.VMEM((ROW, PIECE, HEAD), F32),
        pltpu.VMEM((ROW, PIECE, HEAD), F32),
    ]
    scan_sems = [dma((ROW,)), dma((ROW,)), dma((COLS,)), dma((COLS,)), dma((ROW,)), dma((ROW,))]
    top = pltpu.VMEM((2, H, H), BF16)
    bottom = pltpu.VMEM((2, H, T), BF16)
    square = pltpu.VMEM((W, W), BF16)
    return pl.pallas_call(
        kernel,
        out_shape=(block,) * 4,
        in_specs=[anywhere, anywhere, anywhere, pl.BlockSpec(memory_space=pltpu.VMEM), anywhere],
        out_specs=(anywhere,) * 4,
        scratch_shapes=[low, low, low, low, wide, wide, low, top, bottom, top, bottom, wide, wide]
        + [low] * 4
        + [square, square, pltpu.VMEM((TP, 8, HEAD), F32)]
        + scan_buffers
        + scan_buffers
        + [dma((4,)), dma((4,))]
        + scan_sems
        + scan_sems
        + [dma((TP,)), dma((TP,))],
        compiler_params=pltpu.CompilerParams(
            collective_id=0, has_side_effects=True, vmem_limit_bytes=40 * 1024 * 1024
        ),
    )(queries, keys, values, gain.reshape(1, W), cotangent)


def solution(mesh):
    in_specs = (P("ctx", "tp"), P("ctx", "tp"), P("ctx", "tp"), P("tp"), P("ctx", "tp"))
    out_specs = (P("ctx", "tp"), P("ctx", "tp"), P("ctx", "tp"), P("ctx", "tp"))
    return jax.shard_map(shards, mesh=mesh, in_specs=in_specs, out_specs=out_specs, check_vma=False)
```

```python
import jax
import jax.numpy as jnp
from jax import lax
from jax.experimental import pallas as pl
from jax.experimental.pallas import tpu as pltpu
from jax.sharding import PartitionSpec as P

HEAD = 128
HEADS = 16
D = HEAD * HEADS
ROW = 16
COLS = 4
TP = 8
T = 512
H = T // 2
W = 256
PIECE = 16
epsilon = 1e-06
F32 = jnp.float32
BF16 = jnp.bfloat16
MESH = pl.DeviceIdType.MESH

ROW_ORDER = (8, 7, 9, 6, 10, 5, 11, 4, 12, 3, 13, 2, 14, 1, 15)
COL_ORDER = (2, 1, 3)
TP_ORDER = (4, 3, 5, 2, 6, 1, 7)


def dot(a, b, ca, cb):
    return lax.dot_general(a, b, (((ca,), (cb,)), ((), ())), preferred_element_type=F32)


def kernel(
    q_in, k_in, v_in, gain_in, c_in, n_buf, dq_buf, dk_acc, dv_acc, after_bd, k, v,
    q, c, gain_ref, scaled, att, grad, m_top, m_low, x_top, x_low, prior_bd, stats,
    own_a, gath_a, tot_a, back_a, full_a, own_b, gath_b, tot_b, back_b, full_b,
    in_sem, row_send_a, row_recv_a, col_send_a, col_recv_a, ret_send_a, ret_recv_a,
    row_send_b, row_recv_b, col_send_b, col_recv_b, ret_send_b, ret_recv_b, tp_send, tp_recv,
):
    me = lax.axis_index("ctx")
    z = lax.axis_index("tp")
    x = me // ROW
    r = me % ROW

    loads = [
        pltpu.make_async_copy(src, dst, in_sem.at[i])
        for i, (src, dst) in enumerate(((k_in, k), (v_in, v), (q_in, q), (c_in, c), (gain_in, gain_ref)))
    ]
    for load in loads:
        load.start()

    def row_peer(off):
        j = (r + off) % ROW
        return j, (x * ROW + j, z)

    def col_peer(off):
        return (((x + off) % COLS) * ROW + r, z)

    def tp_peer(off):
        return (me, (z + off) % TP)

    barrier = pltpu.get_barrier_semaphore()
    for off in ROW_ORDER:
        pl.semaphore_signal(barrier, inc=1, device_id=row_peer(off)[1], device_id_type=MESH)
    for off in COL_ORDER:
        pl.semaphore_signal(barrier, inc=1, device_id=col_peer(off), device_id_type=MESH)
    for off in TP_ORDER:
        pl.semaphore_signal(barrier, inc=1, device_id=tp_peer(off), device_id_type=MESH)

    prior_bd[...] = jnp.zeros_like(prior_bd)
    after_bd[...] = jnp.zeros_like(after_bd)

    def put_own(own, left, right):
        state = dot(left, right, 0, 0)
        own[0:HEAD, :] = state[0:HEAD, 0:HEAD]
        own[HEAD:W, :] = state[HEAD:W, HEAD:W]

    def row_copies(own, gath, send, recv):
        copies = []
        for off in ROW_ORDER:
            j, peer = row_peer(off)
            copies.append(
                pltpu.make_async_remote_copy(
                    src_ref=own.at[pl.ds(pl.multiple_of(j * PIECE, PIECE), PIECE)],
                    dst_ref=gath.at[r],
                    send_sem=send.at[off],
                    recv_sem=recv.at[off],
                    device_id=peer,
                    device_id_type=MESH,
                )
            )
        return copies

    def col_copies(tot, send, recv):
        return [
            pltpu.make_async_remote_copy(
                src_ref=tot.at[x],
                dst_ref=tot.at[x],
                send_sem=send.at[off],
                recv_sem=recv.at[off],
                device_id=col_peer(off),
                device_id_type=MESH,
            )
            for off in COL_ORDER
        ]

    def ret_copies(back, full, send, recv):
        copies = []
        for off in ROW_ORDER:
            j, peer = row_peer(off)
            copies.append(
                pltpu.make_async_remote_copy(
                    src_ref=back.at[j],
                    dst_ref=full.at[r],
                    send_sem=send.at[off],
                    recv_sem=recv.at[off],
                    device_id=peer,
                    device_id_type=MESH,
                )
            )
        return copies

    def start(copies):
        for copy in copies:
            copy.start()

    def received(copies):
        for copy in copies:
            copy.wait_recv()

    def sent(copies):
        for copy in copies:
            copy.wait_send()

    def scan_row(own, gath, tot, reverse):
        gath[r] = own[pl.ds(pl.multiple_of(r * PIECE, PIECE), PIECE), :]
        run = jnp.zeros((PIECE, HEAD), F32)
        before = [None] * ROW
        for j in reversed(range(ROW)) if reverse else range(ROW):
            before[j] = run
            run = run + gath[j]
        tot[x] = run
        return before

    def scan_back(before, tot, back, full, reverse):
        base = jnp.zeros((PIECE, HEAD), F32)
        for other in range(COLS):
            counts = (other > x) if reverse else (other < x)
            base = base + jnp.where(counts, tot[other], 0.0)
        for j in range(ROW):
            back[j] = before[j] + base

    loads[0].wait()
    loads[1].wait()
    put_own(own_a, k[...], v[...])
    pl.semaphore_wait(barrier, len(ROW_ORDER) + len(COL_ORDER) + len(TP_ORDER))
    row_a = row_copies(own_a, gath_a, row_send_a, row_recv_a)
    start(row_a)

    loads[2].wait()
    loads[3].wait()
    loads[4].wait()
    lower = lax.broadcasted_iota(jnp.int32, (H, H), 0) >= lax.broadcasted_iota(jnp.int32, (H, H), 1)

    def masked_products(left, right, top, low):
        for h in range(2):
            cols = slice(h * HEAD, (h + 1) * HEAD)
            top[h] = jnp.where(lower, dot(left[0:H, cols], right[0:H, cols], 1, 1), 0.0).astype(BF16)
            low[h, :, 0:H] = dot(left[H:T, cols], right[0:H, cols], 1, 1).astype(BF16)
            low[h, :, H:T] = jnp.where(
                lower, dot(left[H:T, cols], right[H:T, cols], 1, 1), 0.0
            ).astype(BF16)

    masked_products(q, k, m_top, m_low)
    for h in range(2):
        cols = slice(h * HEAD, (h + 1) * HEAD)
        att[0:H, cols] = dot(m_top[h], v[0:H, cols], 1, 0)
        att[H:T, cols] = dot(m_low[h], v[:, cols], 1, 0)
    gain = jnp.concatenate([gain_ref[h:h + 1, :].astype(F32) for h in range(2)], axis=1)
    scaled[...] = c[...].astype(F32) * gain

    received(row_a)
    before = scan_row(own_a, gath_a, tot_a, False)
    col_a = col_copies(tot_a, col_send_a, col_recv_a)
    start(col_a)
    received(col_a)
    scan_back(before, tot_a, back_a, full_a, False)
    ret_a = ret_copies(back_a, full_a, ret_send_a, ret_recv_a)
    start(ret_a)
    full_a[r] = back_a[r]
    received(ret_a)

    def put_bd(bd, full):
        low_state = full[...].reshape(W, HEAD).astype(BF16)
        bd[0:HEAD, 0:HEAD] = low_state[0:HEAD]
        bd[HEAD:W, HEAD:W] = low_state[HEAD:W]

    put_bd(prior_bd, full_a)
    att[...] += dot(q[...], prior_bd[...], 1, 0)

    eye = lax.broadcasted_iota(jnp.int32, (HEAD, HEAD), 0) == lax.broadcasted_iota(
        jnp.int32, (HEAD, HEAD), 1
    )
    rows = []
    for kind in range(2):
        for a in range(T // HEAD):
            part = att[a * HEAD:(a + 1) * HEAD, :]
            other = part if kind == 0 else scaled[a * HEAD:(a + 1) * HEAD, :]
            product = part * other
            sums = jnp.sum(product[:, 0:HEAD] + product[:, HEAD:W], axis=1, keepdims=True)
            rows.append(jnp.sum(jnp.where(eye, sums, 0.0), axis=0, keepdims=True))
    stats[z] = jnp.concatenate(rows, axis=0)
    tp_copies = [
        pltpu.make_async_remote_copy(
            src_ref=stats.at[z],
            dst_ref=stats.at[z],
            send_sem=tp_send.at[off],
            recv_sem=tp_recv.at[off],
            device_id=tp_peer(off),
            device_id_type=MESH,
        )
        for off in TP_ORDER
    ]
    start(tp_copies)
    received(tp_copies)
    totals = jnp.sum(stats[...], axis=0)
    inverse_row = lax.rsqrt(totals[0:4] / D + epsilon)
    coef_row = inverse_row * inverse_row * inverse_row * (totals[4:8] / D)

    def column(row):
        return jnp.sum(jnp.where(eye, row, 0.0), axis=1, keepdims=True)

    inverse = []
    for a in range(T // HEAD):
        span = slice(a * HEAD, (a + 1) * HEAD)
        inverse.append(column(inverse_row[a:a + 1]))
        coef = column(coef_row[a:a + 1])
        grad[span, :] = (inverse[a] * scaled[span, :] - coef * att[span, :]).astype(BF16)

    put_own(own_b, q[...], grad[...])
    row_b = row_copies(own_b, gath_b, row_send_b, row_recv_b)
    start(row_b)

    for a in range(T // HEAD):
        span = slice(a * HEAD, (a + 1) * HEAD)
        n_buf[span, :] = (att[span, :] * inverse[a] * gain).astype(BF16)
    masked_products(grad, v, x_top, x_low)

    received(row_b)
    before = scan_row(own_b, gath_b, tot_b, True)
    col_b = col_copies(tot_b, col_send_b, col_recv_b)
    start(col_b)
    for h in range(2):
        cols = slice(h * HEAD, (h + 1) * HEAD)
        dk_acc[0:H, cols] = dot(x_top[h], q[0:H, cols], 0, 0) + dot(x_low[h, :, 0:H], q[H:T, cols], 0, 0)
        dk_acc[H:T, cols] = dot(x_low[h, :, H:T], q[H:T, cols], 0, 0)
    received(col_b)
    scan_back(before, tot_b, back_b, full_b, True)
    ret_b = ret_copies(back_b, full_b, ret_send_b, ret_recv_b)
    start(ret_b)
    full_b[r] = back_b[r]

    for h in range(2):
        cols = slice(h * HEAD, (h + 1) * HEAD)
        dv_acc[0:H, cols] = dot(m_top[h], grad[0:H, cols], 0, 0) + dot(
            m_low[h, :, 0:H], grad[H:T, cols], 0, 0
        )
        dv_acc[H:T, cols] = dot(m_low[h, :, H:T], grad[H:T, cols], 0, 0)
    for h in range(2):
        cols = slice(h * HEAD, (h + 1) * HEAD)
        from_prior = dot(grad[:, cols], prior_bd[cols, cols], 1, 1)
        dq_buf[0:H, cols] = (dot(x_top[h], k[0:H, cols], 1, 0) + from_prior[0:H]).astype(BF16)
        dq_buf[H:T, cols] = (dot(x_low[h], k[:, cols], 1, 0) + from_prior[H:T]).astype(BF16)
    for copies in (row_a, col_a, ret_a, tp_copies, row_b, col_b):
        sent(copies)

    received(ret_b)
    put_bd(after_bd, full_b)
    sent(ret_b)


def last_kernel(n_buf, dq_buf, dk_acc, dv_acc, after_bd, k, v, n_out, dq_out, dk_out, dv_out, dk_buf, dv_buf, out_sem):
    stores = [
        pltpu.make_async_copy(src, dst, out_sem.at[i])
        for i, (src, dst) in enumerate(((n_buf, n_out), (dq_buf, dq_out), (dk_buf, dk_out), (dv_buf, dv_out)))
    ]
    stores[0].start()
    stores[1].start()
    dk_buf[...] = (dk_acc[...] + dot(v[...], after_bd[...], 1, 1)).astype(BF16)
    stores[2].start()
    dv_buf[...] = (dv_acc[...] + dot(k[...], after_bd[...], 1, 0)).astype(BF16)
    stores[3].start()
    for store in stores:
        store.wait()


def shards(queries, keys, values, gain, cotangent):
    block = jax.ShapeDtypeStruct((T, W), BF16)
    low = pltpu.VMEM((T, W), BF16)
    wide = pltpu.VMEM((T, W), F32)
    dma = pltpu.SemaphoreType.DMA
    scan_buffers = [
        pltpu.VMEM((W, HEAD), F32),
        pltpu.VMEM((ROW, PIECE, HEAD), F32),
        pltpu.VMEM((COLS, PIECE, HEAD), F32),
        pltpu.VMEM((ROW, PIECE, HEAD), F32),
        pltpu.VMEM((ROW, PIECE, HEAD), F32),
    ]
    scan_sems = [dma((ROW,)), dma((ROW,)), dma((COLS,)), dma((COLS,)), dma((ROW,)), dma((ROW,))]
    top = pltpu.VMEM((2, H, H), BF16)
    bottom = pltpu.VMEM((2, H, T), BF16)
    square = pltpu.VMEM((W, W), BF16)
    hbm = pl.BlockSpec(memory_space=pltpu.HBM)
    local = pl.BlockSpec(memory_space=pltpu.VMEM)
    wide_out = jax.ShapeDtypeStruct((T, W), F32)
    queries, keys, values, gain, cotangent = (
        pltpu.with_memory_space_constraint(array, pltpu.HBM)
        for array in (queries, keys, values, gain.reshape(2, HEAD), cotangent)
    )
    kept = pl.pallas_call(
        kernel,
        out_shape=(block, block, wide_out, wide_out, jax.ShapeDtypeStruct((W, W), BF16), block, block),
        in_specs=[hbm] * 5,
        out_specs=(local,) * 7,
        scratch_shapes=[low, low, pltpu.VMEM((2, HEAD), BF16), wide, wide, low, top, bottom, top, bottom, square, pltpu.VMEM((TP, 8, HEAD), F32)]
        + scan_buffers
        + scan_buffers
        + [dma((5,))]
        + scan_sems
        + scan_sems
        + [dma((TP,)), dma((TP,))],
        compiler_params=pltpu.CompilerParams(
            collective_id=0, has_side_effects=True, vmem_limit_bytes=32 * 1024 * 1024
        ),
    )(queries, keys, values, gain, cotangent)
    return pl.pallas_call(
        last_kernel,
        out_shape=(block,) * 4,
        in_specs=[local] * 7,
        out_specs=(hbm,) * 4,
        scratch_shapes=[low, low, dma((4,))],
        compiler_params=pltpu.CompilerParams(vmem_limit_bytes=16 * 1024 * 1024),
    )(*kept)


def solution(mesh):
    in_specs = (P("ctx", "tp"), P("ctx", "tp"), P("ctx", "tp"), P("tp"), P("ctx", "tp"))
    out_specs = (P("ctx", "tp"), P("ctx", "tp"), P("ctx", "tp"), P("ctx", "tp"))
    return jax.shard_map(shards, mesh=mesh, in_specs=in_specs, out_specs=out_specs, check_vma=False)
```

```python
import jax
import jax.numpy as jnp
from jax import lax
from jax.experimental import pallas as pl
from jax.experimental.pallas import tpu as pltpu
from jax.sharding import PartitionSpec as P

HEAD = 128
HEADS = 16
D = HEAD * HEADS
ROW = 16
COLS = 4
TP = 8
T = 512
H = T // 2
W = 256
CHIPS = 8
PIECE = HEAD // CHIPS
epsilon = 1e-06
F32 = jnp.float32
BF16 = jnp.bfloat16
MESH = pl.DeviceIdType.MESH

RING_ORDER = (4, 3, 5, 2, 6, 1, 7)
COL_ORDER = (2, 1, 3)


def dot(a, b, ca, cb):
    return lax.dot_general(a, b, (((ca,), (cb,)), ((), ())), preferred_element_type=F32)


def kernel(
    q_in, k_in, v_in, gain_in, c_in, n_buf, dq_buf, dk_acc, dv_acc, after_bd, k, v,
    q, c_block, gain_ref, scaled, att, grad, m_top, m_low, x_top, x_low, prior_bd, stats,
    own_a, mate_a, chip_a, gath_a, tot_a, back_a, part_a, mess_a, full_a,
    own_b, mate_b, chip_b, gath_b, tot_b, back_b, part_b, mess_b, full_b,
    in_sem, near_a, far_a, ret_a, col_a, near_b, far_b, ret_b, col_b, tp_send, tp_recv,
):
    me = lax.axis_index("ctx")
    z = lax.axis_index("tp")
    x = me // ROW
    y = (me % ROW) // 2
    c = me % 2

    loads = [
        pltpu.make_async_copy(src, dst, in_sem.at[i])
        for i, (src, dst) in enumerate(((k_in, k), (v_in, v), (q_in, q), (c_in, c_block), (gain_in, gain_ref)))
    ]
    for load in loads:
        load.start()

    mate_peer = (me + 1 - 2 * c, z)

    def y_peer(off):
        return (x * ROW + ((y + off) % CHIPS) * 2 + c, z)

    def x_peer(off):
        return (((x + off) % COLS) * ROW + me % ROW, z)

    def tp_peer(off):
        return (me, (z + off) % TP)

    barrier = pltpu.get_barrier_semaphore()
    peers = [mate_peer]
    peers += [y_peer(off) for off in RING_ORDER]
    peers += [x_peer(off) for off in COL_ORDER]
    peers += [tp_peer(off) for off in RING_ORDER]
    for peer in peers:
        pl.semaphore_signal(barrier, inc=1, device_id=peer, device_id_type=MESH)

    prior_bd[...] = jnp.zeros_like(prior_bd)
    after_bd[...] = jnp.zeros_like(after_bd)

    def put_own(own, left, right):
        state = dot(left, right, 0, 0)
        for h in range(2):
            span = slice(h * HEAD, (h + 1) * HEAD)
            own[h] = state[span, span].reshape(CHIPS, PIECE, HEAD)

    def remote(src, dst, send, recv, peer):
        return pltpu.make_async_remote_copy(
            src_ref=src, dst_ref=dst, send_sem=send, recv_sem=recv, device_id=peer, device_id_type=MESH
        )

    def start(copies):
        for copy in copies:
            copy.start()

    def received(copies):
        for copy in copies:
            copy.wait_recv()

    def sent(copies):
        for copy in copies:
            copy.wait_send()

    class Scan:
        def __init__(self, reverse, own, mate, chip, gath, tot, back, part, message, full, near, far, ret, col):
            self.reverse = reverse
            self.own, self.mate, self.chip, self.gath, self.tot = own, mate, chip, gath, tot
            self.back, self.part, self.message, self.full = back, part, message, full
            self.swap = [remote(own.at[1 - c], mate, near.at[0], near.at[1], mate_peer)]
            self.spread = [
                remote(chip.at[(y + off) % CHIPS], gath.at[y], far.at[0, off], far.at[1, off], y_peer(off))
                for off in RING_ORDER
            ]
            self.across = [
                remote(tot.at[x], tot.at[x], col.at[0, off], col.at[1, off], x_peer(off)) for off in COL_ORDER
            ]
            self.gather = [
                remote(back.at[(y + off) % CHIPS], part.at[y], ret.at[0, off], ret.at[1, off], y_peer(off))
                for off in RING_ORDER
            ]
            self.share = [remote(message, full.at[c], near.at[2], near.at[3], mate_peer)]

        def add_chip(self):
            received(self.swap)
            self.chip[...] = self.own[c] + self.mate[...]
            start(self.spread)
            self.gath[y] = self.chip[y]

        def add_row(self):
            received(self.spread)
            run = jnp.zeros((PIECE, HEAD), F32)
            self.before = [None] * CHIPS
            for j in reversed(range(CHIPS)) if self.reverse else range(CHIPS):
                self.before[j] = run
                run = run + self.gath[j]
            self.tot[x] = run
            start(self.across)

        def add_rows(self):
            received(self.across)
            base = jnp.zeros((PIECE, HEAD), F32)
            for other in range(COLS):
                counts = (other > x) if self.reverse else (other < x)
                base = base + jnp.where(counts, self.tot[other], 0.0)
            for j in range(CHIPS):
                self.back[j] = self.before[j] + base
            start(self.gather)
            self.part[y] = self.back[y]

        def exchange(self):
            received(self.gather)
            first = 1 if self.reverse else 0
            self.message[...] = self.part[...] + jnp.where(c == first, self.own[c], 0.0)
            start(self.share)
            self.full[c] = self.part[...] + jnp.where(c == first, 0.0, self.mate[...])

        def finish(self, block_diagonal):
            received(self.share)
            for h in range(2):
                span = slice(h * HEAD, (h + 1) * HEAD)
                block_diagonal[span, span] = self.full[h].reshape(HEAD, HEAD).astype(BF16)

        def drain(self):
            for copies in (self.swap, self.spread, self.across, self.gather, self.share):
                sent(copies)

    fore = Scan(False, own_a, mate_a, chip_a, gath_a, tot_a, back_a, part_a, mess_a, full_a, near_a, far_a, ret_a, col_a)
    aft = Scan(True, own_b, mate_b, chip_b, gath_b, tot_b, back_b, part_b, mess_b, full_b, near_b, far_b, ret_b, col_b)

    loads[0].wait()
    loads[1].wait()
    put_own(own_a, k[...], v[...])
    pl.semaphore_wait(barrier, len(peers))
    start(fore.swap)

    loads[2].wait()
    loads[3].wait()
    loads[4].wait()
    lower = lax.broadcasted_iota(jnp.int32, (H, H), 0) >= lax.broadcasted_iota(jnp.int32, (H, H), 1)

    def masked_products(left, right, top, low):
        for h in range(2):
            cols = slice(h * HEAD, (h + 1) * HEAD)
            top[h] = jnp.where(lower, dot(left[0:H, cols], right[0:H, cols], 1, 1), 0.0).astype(BF16)
            low[h, :, 0:H] = dot(left[H:T, cols], right[0:H, cols], 1, 1).astype(BF16)
            low[h, :, H:T] = jnp.where(
                lower, dot(left[H:T, cols], right[H:T, cols], 1, 1), 0.0
            ).astype(BF16)

    gain = jnp.concatenate([gain_ref[h:h + 1, :].astype(F32) for h in range(2)], axis=1)
    scaled[...] = c_block[...].astype(F32) * gain
    fore.add_chip()
    masked_products(q, k, m_top, m_low)
    for h in range(2):
        cols = slice(h * HEAD, (h + 1) * HEAD)
        att[0:H, cols] = dot(m_top[h], v[0:H, cols], 1, 0)
        att[H:T, cols] = dot(m_low[h], v[:, cols], 1, 0)
    fore.add_row()
    fore.add_rows()
    fore.exchange()
    fore.finish(prior_bd)
    att[...] += dot(q[...], prior_bd[...], 1, 0)

    eye = lax.broadcasted_iota(jnp.int32, (HEAD, HEAD), 0) == lax.broadcasted_iota(
        jnp.int32, (HEAD, HEAD), 1
    )
    rows = []
    for kind in range(2):
        for a in range(T // HEAD):
            part = att[a * HEAD:(a + 1) * HEAD, :]
            other = part if kind == 0 else scaled[a * HEAD:(a + 1) * HEAD, :]
            product = part * other
            sums = jnp.sum(product[:, 0:HEAD] + product[:, HEAD:W], axis=1, keepdims=True)
            rows.append(jnp.sum(jnp.where(eye, sums, 0.0), axis=0, keepdims=True))
    stats[z] = jnp.concatenate(rows, axis=0)
    tp_copies = [
        pltpu.make_async_remote_copy(
            src_ref=stats.at[z],
            dst_ref=stats.at[z],
            send_sem=tp_send.at[off],
            recv_sem=tp_recv.at[off],
            device_id=tp_peer(off),
            device_id_type=MESH,
        )
        for off in RING_ORDER
    ]
    start(tp_copies)
    received(tp_copies)
    totals = jnp.sum(stats[...], axis=0)
    inverse_row = lax.rsqrt(totals[0:4] / D + epsilon)
    coef_row = inverse_row * inverse_row * inverse_row * (totals[4:8] / D)

    def column(row):
        return jnp.sum(jnp.where(eye, row, 0.0), axis=1, keepdims=True)

    inverse = []
    for a in range(T // HEAD):
        span = slice(a * HEAD, (a + 1) * HEAD)
        inverse.append(column(inverse_row[a:a + 1]))
        coef = column(coef_row[a:a + 1])
        grad[span, :] = (inverse[a] * scaled[span, :] - coef * att[span, :]).astype(BF16)

    put_own(own_b, q[...], grad[...])
    start(aft.swap)

    for a in range(T // HEAD):
        span = slice(a * HEAD, (a + 1) * HEAD)
        n_buf[span, :] = (att[span, :] * inverse[a] * gain).astype(BF16)
    aft.add_chip()
    masked_products(grad, v, x_top, x_low)
    for h in range(2):
        cols = slice(h * HEAD, (h + 1) * HEAD)
        dk_acc[0:H, cols] = dot(x_top[h], q[0:H, cols], 0, 0) + dot(x_low[h, :, 0:H], q[H:T, cols], 0, 0)
        dk_acc[H:T, cols] = dot(x_low[h, :, H:T], q[H:T, cols], 0, 0)
    aft.add_row()
    for h in range(2):
        cols = slice(h * HEAD, (h + 1) * HEAD)
        dv_acc[0:H, cols] = dot(m_top[h], grad[0:H, cols], 0, 0) + dot(
            m_low[h, :, 0:H], grad[H:T, cols], 0, 0
        )
        dv_acc[H:T, cols] = dot(m_low[h, :, H:T], grad[H:T, cols], 0, 0)
    aft.add_rows()
    for h in range(2):
        cols = slice(h * HEAD, (h + 1) * HEAD)
        from_prior = dot(grad[:, cols], prior_bd[cols, cols], 1, 1)
        dq_buf[0:H, cols] = (dot(x_top[h], k[0:H, cols], 1, 0) + from_prior[0:H]).astype(BF16)
        dq_buf[H:T, cols] = (dot(x_low[h], k[:, cols], 1, 0) + from_prior[H:T]).astype(BF16)
    fore.drain()
    sent(tp_copies)
    aft.exchange()
    aft.finish(after_bd)
    aft.drain()


def last_kernel(n_buf, dq_buf, dk_acc, dv_acc, after_bd, k, v, n_out, dq_out, dk_out, dv_out, dk_buf, dv_buf, out_sem):
    stores = [
        pltpu.make_async_copy(src, dst, out_sem.at[i])
        for i, (src, dst) in enumerate(((n_buf, n_out), (dq_buf, dq_out), (dk_buf, dk_out), (dv_buf, dv_out)))
    ]
    stores[0].start()
    stores[1].start()
    dk_buf[...] = (dk_acc[...] + dot(v[...], after_bd[...], 1, 1)).astype(BF16)
    stores[2].start()
    dv_buf[...] = (dv_acc[...] + dot(k[...], after_bd[...], 1, 0)).astype(BF16)
    stores[3].start()
    for store in stores:
        store.wait()


def shards(queries, keys, values, gain, cotangent):
    block = jax.ShapeDtypeStruct((T, W), BF16)
    low = pltpu.VMEM((T, W), BF16)
    wide = pltpu.VMEM((T, W), F32)
    dma = pltpu.SemaphoreType.DMA
    pieces = pltpu.VMEM((CHIPS, PIECE, HEAD), F32)
    both = pltpu.VMEM((2, CHIPS, PIECE, HEAD), F32)
    scan_buffers = [both, pieces, pieces, pieces, pltpu.VMEM((COLS, PIECE, HEAD), F32), pieces, pieces, pieces, both]
    scan_sems = [dma((4,)), dma((2, CHIPS)), dma((2, CHIPS)), dma((2, COLS))]
    top = pltpu.VMEM((2, H, H), BF16)
    bottom = pltpu.VMEM((2, H, T), BF16)
    square = pltpu.VMEM((W, W), BF16)
    hbm = pl.BlockSpec(memory_space=pltpu.HBM)
    local = pl.BlockSpec(memory_space=pltpu.VMEM)
    wide_out = jax.ShapeDtypeStruct((T, W), F32)
    queries, keys, values, gain, cotangent = (
        pltpu.with_memory_space_constraint(array, pltpu.HBM)
        for array in (queries, keys, values, gain.reshape(2, HEAD), cotangent)
    )
    kept = pl.pallas_call(
        kernel,
        out_shape=(block, block, wide_out, wide_out, jax.ShapeDtypeStruct((W, W), BF16), block, block),
        in_specs=[hbm] * 5,
        out_specs=(local,) * 7,
        scratch_shapes=[low, low, pltpu.VMEM((2, HEAD), BF16), wide, wide, low, top, bottom, top, bottom, square, pltpu.VMEM((TP, 8, HEAD), F32)]
        + scan_buffers
        + scan_buffers
        + [dma((5,))]
        + scan_sems
        + scan_sems
        + [dma((TP,)), dma((TP,))],
        compiler_params=pltpu.CompilerParams(
            collective_id=0, has_side_effects=True, vmem_limit_bytes=32 * 1024 * 1024
        ),
    )(queries, keys, values, gain, cotangent)
    return pl.pallas_call(
        last_kernel,
        out_shape=(block,) * 4,
        in_specs=[local] * 7,
        out_specs=(hbm,) * 4,
        scratch_shapes=[low, low, dma((4,))],
        compiler_params=pltpu.CompilerParams(vmem_limit_bytes=16 * 1024 * 1024),
    )(*kept)


def solution(mesh):
    in_specs = (P("ctx", "tp"), P("ctx", "tp"), P("ctx", "tp"), P("tp"), P("ctx", "tp"))
    out_specs = (P("ctx", "tp"), P("ctx", "tp"), P("ctx", "tp"), P("ctx", "tp"))
    return jax.shard_map(shards, mesh=mesh, in_specs=in_specs, out_specs=out_specs, check_vma=False)
```
